256 devices in a mesh: grp: 4 (over z_lo), gx: 16 (over y, z_hi, core), gy: 4 (over x).
Axes of the slice: x: 4, y: 4, z: 8 (z_hi: 2, z_lo: 4; z = z_hi * 4 + z_lo), core: 2. Of those that a mesh axis runs over, the one named last changes fastest.
Arguments:
- checkpoint: float32 [2, 2, 2, 256, 64, 256], P(None, None, None, 'gx', 'gy'), may hold values from -6 to 6
- courant: float32 [256, 64, 256], P('gx', 'gy'), may hold values from 0.03 to 0.15
- epsilon: float32 [256, 64, 256], P('gx', 'gy'), may hold values from 0.3 to 0.6
- delta: float32 [256, 64, 256], P('gx', 'gy'), may hold values from 0.05 to 0.3
- positions: int32 [4, 3, 512], replicated, may hold values from 0 to 255, as said below
- amplitudes: float32 [4, 16, 512], replicated, may hold values from -6 to 6
- offsets: int32 [16], replicated, may hold values from -8 to 8, as said below
Outputs:
- image: float32 [16, 256, 64, 256], P('grp', 'gx', 'gy')
The draws below stay inside these ranges and needn't reach their ends.
Inputs may be any that keep to these rules, and one draw needn't show every extreme that they name: `positions`: each column of a row is a cell inside the grid: x below 256, y below 64, z below 256. `offsets`: both -8 and 8 occur.
All inputs are finite; a program needn't handle non-finite values.
Results may differ from the reference program's by a relative error of at most 0.0003.
Values sent between devices are 32-bit elements; how exact they have to be, the bound alone decides.
No kernel may reach another device: no remote copies, remote signals or barrier semaphores. Data moves between devices by JAX's collectives and lax.ppermute only.
A program may use at most 128 MiB of HBM per device.

```python
import math
import jax
import jax.numpy as jnp
from jax import lax

NZ = 256
NREC = 512
NSTEPS = 16
SNAP = 4
HMAX = 8
NH = 16
GROUPS = 4
SHOTS = 2
NX = 256
NY = 64


def draw_positions(key, part):
    key_x, key_y, key_z = jax.random.split(jax.random.fold_in(key, 11), 3)
    shape = (GROUPS, NREC)
    coord_x = jax.random.randint(key_x, shape, 0, NX)
    coord_y = jax.random.randint(key_y, shape, 0, NY)
    coord_z = jax.random.randint(key_z, shape, 0, NZ)
    return jnp.stack([coord_x, coord_y, coord_z], 1).astype(jnp.int32)


def draw_offsets(key, part):
    key_vals, key_perm = jax.random.split(jax.random.fold_in(key, 23))
    values = jax.random.randint(key_vals, (NH,), -HMAX, HMAX + 1)
    order = jax.random.permutation(key_perm, NH)
    values = values.at[order[0]].set(HMAX).at[order[1]].set(-HMAX)
    return values.astype(jnp.int32)


def levels(rng, dims, cuts, low, high):
    level, own = 1.0, jax.random.fold_in(rng, 6)
    for dim, parts in cuts:
        steps = jnp.exp(jax.random.uniform(jax.random.fold_in(own, dim), (parts,), jnp.float32, low / len(cuts), high / len(cuts)))
        level = level * jnp.repeat(steps, dims[dim] // parts).reshape([-1 if axis == dim else 1 for axis in range(len(dims))])
    return level


def noise(own_key, dims, width, limit, cuts=(), dtype=jnp.bfloat16):
    factor_of = levels(own_key, dims, cuts, -0.22, 0.18) if cuts else 1.0
    entries = jax.random.normal(own_key, dims, jnp.float32) * width * factor_of
    return jnp.minimum(jnp.maximum(entries, -limit), limit).astype(dtype)


def setup_inputs(seed: int = 0) -> dict:
    streams_of = jax.random.split(jax.random.key(seed), 8)
    checkpoint = noise(streams_of[0], (SHOTS, 2, 2, NX, NY, NZ), 1.0, 6.0, ((3, 16), (4, 4)), jnp.float32)
    courant = jnp.clip(jnp.exp(math.log(0.15) - 1.609438 * jax.random.uniform(streams_of[1], (NX, NY, NZ), jnp.float32) ** levels(streams_of[1], (NX, NY, NZ), ((0, 16), (1, 4)), -0.2, 0.2)), 0.03, 0.15)
    epsilon = jnp.clip(0.3 + 0.3 * jax.random.uniform(streams_of[2], (NX, NY, NZ), jnp.float32) ** levels(streams_of[2], (NX, NY, NZ), ((0, 16), (1, 4)), -0.2, 0.2), 0.3, 0.6)
    delta = jnp.clip(0.05 + 0.25 * jax.random.uniform(streams_of[3], (NX, NY, NZ), jnp.float32) ** levels(streams_of[3], (NX, NY, NZ), ((0, 16), (1, 4)), -0.2, 0.2), 0.05, 0.3)
    positions = draw_positions(jax.random.fold_in(streams_of[7], 71), 0)
    amplitudes = noise(streams_of[5], (GROUPS, NSTEPS, NREC), 1.0, 6.0, (), jnp.float32)
    offsets = draw_offsets(jax.random.fold_in(streams_of[7], 71), 0)
    return dict(checkpoint=checkpoint, courant=courant, epsilon=epsilon, delta=delta, positions=positions, amplitudes=amplitudes, offsets=offsets)


def laplacians(main_field, aux_field):
    padded = jnp.pad(main_field, ((1, 1), (1, 1), (0, 0)))
    across = padded[2:, 1:-1] + padded[:-2, 1:-1] + padded[1:-1, 2:] + padded[1:-1, :-2] - 4.0 * main_field
    deep_pad = jnp.pad(aux_field, ((0, 0), (0, 0), (1, 1)))
    vertical = deep_pad[:, :, 2:] + deep_pad[:, :, :-2] - 2.0 * aux_field
    return (across, vertical)

def replay(current, previous, coefs, coords, strengths):
    flat_index = ((coords[0] * NY + coords[1]) * NZ + coords[2]).astype(jnp.int32)
    snapshots = []
    for moment in range(NSTEPS):
        across, vertical = laplacians(current[0], current[1])
        source = jnp.zeros((NX * NY * NZ,), jnp.float32).at[flat_index].add(strengths[moment]).reshape(NX, NY, NZ)
        main_next = 2.0 * current[0] - previous[0] + coefs[0] * across + coefs[1] * vertical + source
        aux_next = 2.0 * current[1] - previous[1] + coefs[1] * across + coefs[2] * vertical + source
        previous = current
        current = jnp.stack([main_next, aux_next])
        if (moment + 1) % SNAP == 0:
            snapshots.append(current[0])
    return snapshots

def reference(checkpoint, courant, epsilon, delta, positions, amplitudes, offsets):
    coefs = jnp.stack([courant + 2.0 * courant * epsilon, courant * jnp.sqrt(2.0 * delta + 1.0), courant])
    zero_state = jnp.zeros_like(checkpoint[0, 0])
    pairs = []
    for shot in range(SHOTS):
        source_snaps = replay(checkpoint[shot, 0], checkpoint[shot, 1], coefs, positions[2 * shot], amplitudes[2 * shot])
        receiver_snaps = replay(zero_state, zero_state, coefs, positions[2 * shot + 1], amplitudes[2 * shot + 1])
        pairs.append((source_snaps, receiver_snaps))
    margins = ((HMAX, HMAX), (0, 0), (0, 0))

    def one_offset(shift):
        total = jnp.zeros((NX, NY, NZ), jnp.float32)
        for source_snaps, receiver_snaps in pairs:
            for number in range(len(source_snaps)):
                padded_source = jnp.pad(source_snaps[number], margins)
                shifted_source = lax.dynamic_slice_in_dim(padded_source, (HMAX - shift).astype(jnp.int32), NX, 0)
                padded_recv = jnp.pad(receiver_snaps[number], margins)
                shifted_recv = lax.dynamic_slice_in_dim(padded_recv, (HMAX + shift).astype(jnp.int32), NX, 0)
                total = total + shifted_source * shifted_recv
        return total
    return lax.map(one_offset, offsets)
```

```python
import functools

import jax
import jax.numpy as jnp
from jax import lax
from jax.experimental import pallas as pl
from jax.experimental.pallas import tpu as pltpu
from jax.sharding import PartitionSpec as P

NSTEPS = 16
SNAP = 4
HMAX = 8
BLOCKS = NSTEPS // SNAP
NW = 2
LANES = 128
TILE = 16
EXT = TILE + 2 * SNAP
YPAD = 8
YROWS = EXT + 2 * YPAD
FIELDS = ((0, 4, 0), (1, 3, 4), (2, 3, 7), (3, 2, 10))
ROWS = 12
CROWS = 9
PARITY, LEFT, RIGHT, LOW, HIGH, START, FIRST, CHUNK, GROUP = range(9)

VM = pl.BlockSpec(memory_space=pltpu.VMEM)
SM = pl.BlockSpec(memory_space=pltpu.SMEM)
F32 = jnp.float32


def struct(*shape, dtype=F32):
    return jax.ShapeDtypeStruct(shape, dtype)


def call(kernel, name, outs, in_specs, scratch=(), out_specs=None, cost=2_000_000):
    return pl.pallas_call(
        kernel,
        out_shape=outs,
        in_specs=in_specs,
        out_specs=out_specs if out_specs is not None else jax.tree.map(lambda _: VM, outs),
        scratch_shapes=list(scratch),
        compiler_params=pltpu.CompilerParams(vmem_limit_bytes=40 << 20),
        cost_estimate=pl.CostEstimate(flops=cost, bytes_accessed=cost, transcendentals=0),
        name=name,
    )


def lane_iota(rows=8):
    return lax.broadcasted_iota(jnp.int32, (rows, LANES), 1)


def strips(info, state, width, rows, first, second):
    even = 1 - info[PARITY]
    far = TILE - width
    first[rows : rows + width] = state[pl.ds(even * far, width)]
    second[rows : rows + width] = state[pl.ds((1 - even) * far, width)]


def sides(info, first, second, row):
    odd = info[PARITY] == 1
    a, b = first[row], second[row]
    left = jnp.where(odd, a, b)
    right = jnp.where(odd, b, a)
    zero = jnp.zeros_like(a)
    return jnp.where(info[LEFT] == 1, left, zero), jnp.where(info[RIGHT] == 1, right, zero)


def prepare(info, check, courant, epsilon, delta, state, coef, s1, s2, c1, c2):
    start = info[START]
    shift = lax.rem(LANES - start, LANES)
    low = lane_iota(TILE) < LANES - start

    def window(block):
        return jnp.where(
            low,
            pltpu.roll(block[:, :LANES], shift, 1),
            pltpu.roll(block[:, LANES:], shift, 1),
        )

    def layer(x, carry):
        c = window(courant[x])
        e = window(epsilon[x])
        d = window(delta[x])
        coef[0, x] = c + 2.0 * c * e
        coef[1, x] = c * jnp.sqrt(2.0 * d + 1.0)
        coef[2, x] = c
        for w in range(NW):
            for f in range(4):
                state[w, f, x] = window(check[w, f // 2, f % 2, x])
        return carry

    lax.fori_loop(0, TILE, layer, 0)
    for k in range(3):
        strips(info, coef.at[k], 3, 3 * k, c1, c2)
    for w in range(NW):
        for f, width, row in FIELDS:
            strips(info, state.at[w, f], width, w * ROWS + row, s1, s2)


def listing(code, cells, points, count):
    for row in range(code.shape[0]):

        def one(i, n):
            value = code[row, i]
            cells[row, n] = value
            points[row, n] = i
            return n + jnp.where(value >= 0, 1, 0)

        count[row] = lax.fori_loop(0, code.shape[1], one, jnp.int32(0), unroll=8)


def coef_rows(info, coef, r1, r2, low, high):
    for k in range(3):
        for row in range(3):
            left, right = sides(info, r1, r2, 3 * k + row)
            for x, layer in ((1 + row, left), (SNAP + TILE + row, right)):
                low[x * CROWS + 3 * k : x * CROWS + 3 * k + 3] = layer[:3]
                high[x * CROWS + 3 * k : x * CROWS + 3 * k + 3] = layer[TILE - 3 :]
        for x in range(TILE):
            at = (x + SNAP) * CROWS + 3 * k
            low[at : at + 3] = coef[k, x, :3]
            high[at : at + 3] = coef[k, x, TILE - 3 :]
    blank = jnp.zeros((CROWS, LANES), F32)
    for x in (0, EXT - 1):
        low[x * CROWS : (x + 1) * CROWS] = blank
        high[x * CROWS : (x + 1) * CROWS] = blank


def coef_whole(info, coef, r1, r2, below, above, out):
    out[...] = jnp.zeros_like(out)
    for k in range(3):
        out[k, SNAP : SNAP + TILE, SNAP : SNAP + TILE] = coef[k]
        for row in range(3):
            left, right = sides(info, r1, r2, 3 * k + row)
            out[k, 1 + row, SNAP : SNAP + TILE] = left
            out[k, SNAP + TILE + row, SNAP : SNAP + TILE] = right
        for x in range(1, EXT - 1):
            at = x * CROWS + 3 * k
            lo = below[at : at + 3]
            hi = above[at : at + 3]
            out[k, x, 1:4] = jnp.where(info[LOW] == 1, lo, jnp.zeros_like(lo))
            out[k, x, SNAP + TILE : SNAP + TILE + 3] = jnp.where(info[HIGH] == 1, hi, jnp.zeros_like(hi))


def field_rows(info, state, r1, r2, low, high):
    for w in range(NW):
        for f, width, row in FIELDS:
            at = w * ROWS + row
            low[SNAP : SNAP + TILE, at : at + width] = state[w, f, :, :width]
            high[SNAP : SNAP + TILE, at : at + width] = state[w, f, :, TILE - width :]
            for n in range(width):
                left, right = sides(info, r1, r2, at + n)
                for x, layer in ((SNAP - width + n, left), (SNAP + TILE + n, right)):
                    low[x, at : at + width] = layer[:width]
                    high[x, at : at + width] = layer[TILE - width :]
            for x in [*range(SNAP - width), *range(EXT - SNAP + width, EXT)]:
                low[x, at : at + width] = jnp.zeros((width, LANES), F32)
                high[x, at : at + width] = jnp.zeros((width, LANES), F32)


def block_kernel(rows, has_state, last, *refs):
    refs = list(refs)
    info, cells, points, count, amps, coef = refs[:6]
    refs = refs[6:]
    if has_state:
        state, r1, r2, below, above = refs[:5]
        refs = refs[5:]
    if not last:
        out_state, s1, s2 = refs[:3]
        refs = refs[3:]
    snap, n1, n2 = refs[:3]
    bufs = refs[3:]
    own = slice(YPAD + SNAP, YPAD + SNAP + TILE)
    if has_state:
        for w in range(NW):
            for f, width, row in FIELDS:
                at = w * ROWS + row
                bufs[f][w, SNAP : SNAP + TILE, own] = state[w, f]
                for n in range(width):
                    left, right = sides(info, r1, r2, at + n)
                    bufs[f][w, SNAP - width + n, own] = left
                    bufs[f][w, SNAP + TILE + n, own] = right
                for x in range(SNAP - width, SNAP + TILE + width):
                    lo = below[x, at : at + width]
                    hi = above[x, at : at + width]
                    bufs[f][w, x, YPAD + SNAP - width : YPAD + SNAP] = jnp.where(
                        info[LOW] == 1, lo, jnp.zeros_like(lo)
                    )
                    bufs[f][w, x, YPAD + SNAP + TILE : YPAD + SNAP + TILE + width] = jnp.where(
                        info[HIGH] == 1, hi, jnp.zeros_like(hi)
                    )
    else:
        for buf in bufs:
            buf[...] = jnp.zeros_like(buf)

    lanes = lane_iota()
    bottom, top = lanes == 0, lanes == LANES - 1
    one_row = lane_iota(1)
    for step in range(SNAP):
        extent = SNAP - 1 - step
        now, then = (bufs[:2], bufs[2:]) if step % 2 == 0 else (bufs[2:], bufs[:2])
        main, aux = now
        main_next, aux_next = then

        def layer(x, carry):
            for chunk in range(EXT // 8):
                at = YPAD + 8 * chunk
                mid = pl.ds(at, 8)
                horizontal = coef[0, x, 8 * chunk : 8 * chunk + 8]
                coupling = coef[1, x, 8 * chunk : 8 * chunk + 8]
                vertical = coef[2, x, 8 * chunk : 8 * chunk + 8]
                for w in range(NW):
                    m = main[w, x, mid]
                    across = (
                        (main[w, x + 1, mid] + main[w, x - 1, mid])
                        + (main[w, x, pl.ds(at + 1, 8)] + main[w, x, pl.ds(at - 1, 8)])
                        - 4.0 * m
                    )
                    a = aux[w, x, mid]
                    deeper = jnp.where(top, 0.0, pltpu.roll(a, LANES - 1, 1))
                    upper = jnp.where(bottom, 0.0, pltpu.roll(a, 1, 1))
                    down = deeper + upper - 2.0 * a
                    main_next[w, x, mid] = (
                        2.0 * m - main_next[w, x, mid] + (horizontal * across + coupling * down)
                    )
                    aux_next[w, x, mid] = (
                        2.0 * a - aux_next[w, x, mid] + (coupling * across + vertical * down)
                    )
            return carry

        lax.fori_loop(SNAP - extent, SNAP + TILE + extent, layer, 0)
        for w in range(NW):

            def inject(i, carry):
                cell = cells[rows[w], i]
                amount = amps[w, step, points[rows[w], i]]
                x = lax.shift_right_logical(cell, 16)
                y = lax.bitwise_and(lax.shift_right_logical(cell, 8), 255)
                z = lax.bitwise_and(cell, 255)
                add = jnp.where(one_row == z, amount, 0.0)
                main_next[w, x, pl.ds(y, 1)] += add
                aux_next[w, x, pl.ds(y, 1)] += add
                return carry

            lax.fori_loop(0, count[rows[w]], inject, 0)

    first = info[FIRST]
    left_half = lane_iota(TILE) < LANES // 2
    to_left = lax.rem(LANES - first, LANES)
    to_right = lax.rem(LANES + LANES // 2 - first, LANES)

    def finish(x, carry):
        if not last:
            for w in range(NW):
                for f in range(4):
                    out_state[w, f, x] = bufs[f][w, x + SNAP, own]
        snap[x] = jnp.where(
            left_half,
            pltpu.roll(bufs[0][0, x + SNAP, own], to_left, 1),
            pltpu.roll(bufs[0][1, x + SNAP, own], to_right, 1),
        )
        return carry

    lax.fori_loop(0, TILE, finish, 0)
    strips(info, snap, HMAX, 0, n1, n2)
    if not last:
        for w in range(NW):
            for f, width, row in FIELDS:
                strips(info, out_state.at[w, f], width, w * ROWS + row, s1, s2)


def widen(info, own, r1, r2, out):
    out[HMAX : HMAX + TILE] = own[...]
    for row in range(HMAX):
        left, right = sides(info, r1, r2, row)
        out[row] = left
        out[HMAX + TILE + row] = right


def image_kernel(count, first, *refs):
    refs = list(refs)
    info, offsets = refs[:2]
    refs = refs[2:]
    if not first:
        before, refs = refs[0], refs[1:]
    snaps, refs = refs[: 6 * count], refs[6 * count :]
    outs, (source, receiver) = refs[:-2], refs[-2:]
    for j in range(count):
        widen(info, *snaps[6 * j : 6 * j + 3], source.at[j])
        widen(info, *snaps[6 * j + 3 : 6 * j + 6], receiver.at[j])
    half = lane_iota() < LANES // 2
    group = info[GROUP]
    for d in range(4):
        for i in range(4):
            shift = offsets[4 * lax.bitwise_xor(group, d) + i]

            def layer(x, carry):
                at_source = x + HMAX - shift
                at_receiver = x + HMAX + shift
                sums = []
                for y in range(2):
                    rows = pl.ds(8 * y, 8)
                    total = source[0, at_source, rows] * receiver[0, at_receiver, rows]
                    for j in range(1, count):
                        total += source[j, at_source, rows] * receiver[j, at_receiver, rows]
                    if not first:
                        total += before[4 * d + i, x, rows]
                    sums.append(total)
                if first:
                    for y in range(2):
                        outs[0][4 * d + i, x, 8 * y : 8 * y + 8] = sums[y]
                else:
                    a, b = (s + pltpu.roll(s, LANES // 2, 1) for s in sums)
                    outs[d][i, x] = jnp.where(half, a, b)
                return carry

            lax.fori_loop(0, TILE, layer, 0, unroll=2)


def gather_kernel(info, *refs):
    parts, out, held = refs[:4], refs[4], refs[5]
    for d in range(4):
        held[d] = parts[d][...]
    half = lane_iota() < LANES // 2
    mine = info[CHUNK]
    for tile in range(2):
        low = lax.bitwise_xor(mine, 2 * tile)
        high = lax.bitwise_xor(mine, 2 * tile + 1)
        for i in range(4):

            def layer(x, carry):
                a = held[low, i, x]
                b = held[high, i, x]
                at = pl.ds(tile * LANES, LANES)
                out[i, x, 0:8, at] = jnp.where(half, a, pltpu.roll(b, LANES // 2, 1))
                out[i, x, 8:16, at] = jnp.where(half, pltpu.roll(a, LANES // 2, 1), b)
                return carry

            lax.fori_loop(0, TILE, layer, 0, unroll=2)


def shards(checkpoint, courant, epsilon, delta, positions, amplitudes, offsets):
    group, gx, gy = (lax.axis_index(axis) for axis in ("grp", "gx", "gy"))
    groups, nx, ny = (lax.axis_size(axis) for axis in ("grp", "gx", "gy"))
    quarter = courant.shape[2] // groups
    chunk = group
    start = jnp.clip(quarter * chunk - quarter // 2, 0, courant.shape[2] - LANES)
    info = jnp.stack(
        [
            gx % 2,
            (gx > 0).astype(jnp.int32),
            (gx < nx - 1).astype(jnp.int32),
            (gy > 0).astype(jnp.int32),
            (gy < ny - 1).astype(jnp.int32),
            start,
            quarter * chunk - start,
            chunk,
            group,
        ]
    ).astype(jnp.int32)

    pair = [(i, i ^ 1) for i in range(nx)]
    other = [(i, ((i - 1) % nx ^ 1) + 1) for i in range(nx)]
    other = [(i, j % nx) for i, j in other]

    def swap_x(first, second):
        return lax.ppermute(first, "gx", pair), lax.ppermute(second, "gx", other)

    def swap_y(low, high):
        below = lax.ppermute(high, "gy", [(i, (i + 1) % ny) for i in range(ny)])
        above = lax.ppermute(low, "gy", [(i, (i - 1) % ny) for i in range(ny)])
        return below, above

    state, coef, s1, s2, c1, c2 = call(
        prepare,
        "prepare",
        (
            struct(NW, 4, TILE, TILE, LANES),
            struct(3, TILE, TILE, LANES),
            struct(NW * ROWS, TILE, LANES),
            struct(NW * ROWS, TILE, LANES),
            struct(CROWS, TILE, LANES),
            struct(CROWS, TILE, LANES),
        ),
        [SM, VM, VM, VM, VM],
    )(info, checkpoint, courant, epsilon, delta)
    c1, c2 = swap_x(c1, c2)
    r1, r2 = swap_x(s1, s2)

    local_x = positions[:, 0] - gx * TILE + SNAP
    local_y = positions[:, 1] - gy * TILE + SNAP
    local_z = positions[:, 2] - start
    inside = (local_x >= 1) & (local_x < EXT - 1) & (local_y >= 1) & (local_y < EXT - 1)
    inside &= (local_z >= 0) & (local_z < LANES)
    code = jnp.where(inside, (local_x << 16) | ((local_y + YPAD) << 8) | local_z, -1)
    rows, npoints = code.shape
    lists = call(
        listing,
        "listing",
        (
            struct(rows, npoints, dtype=jnp.int32),
            struct(rows, npoints, dtype=jnp.int32),
            struct(rows, dtype=jnp.int32),
        ),
        [SM],
        out_specs=(SM, SM, SM),
    )(code)

    low, high = call(
        coef_rows,
        "coef_rows",
        (struct(EXT * CROWS, LANES), struct(EXT * CROWS, LANES)),
        [SM, VM, VM, VM],
    )(info, coef, c1, c2)
    below, above = swap_y(low, high)
    coef = call(coef_whole, "coef_whole", struct(3, EXT, EXT, LANES), [SM] + [VM] * 5)(
        info, coef, c1, c2, below, above
    )

    def exchange(state, r1, r2):
        low, high = call(
            field_rows,
            "field_rows",
            (struct(EXT, NW * ROWS, LANES), struct(EXT, NW * ROWS, LANES)),
            [SM, VM, VM, VM],
        )(info, state, r1, r2)
        return (state, r1, r2, *swap_y(low, high))

    def run_block(number, chain, halo):
        last = number == BLOCKS - 1
        amps = amplitudes[chain::2, number * SNAP : (number + 1) * SNAP]
        outs = [struct(TILE, TILE, LANES)] + [struct(HMAX, TILE, LANES)] * 2
        if not last:
            outs = [
                struct(NW, 4, TILE, TILE, LANES),
                struct(NW * ROWS, TILE, LANES),
                struct(NW * ROWS, TILE, LANES),
            ] + outs
        return call(
            functools.partial(block_kernel, (chain, chain + 2), bool(halo), last),
            "block",
            tuple(outs),
            [SM] * 5 + [VM] * (1 + len(halo)),
            scratch=[pltpu.VMEM((NW, EXT, YROWS, LANES), F32)] * 4,
            cost=8_000_000,
        )(info, *lists, amps, coef, *halo)

    snaps = []
    halos = [exchange(state, r1, r2), ()]
    for number in range(BLOCKS):
        pieces = []
        for chain in (1, 0):
            outs = run_block(number, chain, halos[chain])
            if number < BLOCKS - 1:
                state, s1, s2 = outs[:3]
                halos[chain] = exchange(state, *swap_x(s1, s2))
                outs = outs[3:]
            pieces = [outs[0], *swap_x(*outs[1:])] + pieces
        snaps.append(pieces)

    noffsets = offsets.shape[0]
    wide = [TILE + 2 * HMAX, TILE, LANES]
    partial = call(
        functools.partial(image_kernel, BLOCKS - 1, True),
        "image",
        (struct(noffsets, TILE, TILE, LANES),),
        [SM, SM] + [VM] * (6 * (BLOCKS - 1)),
        scratch=[pltpu.VMEM((BLOCKS - 1, *wide), F32)] * 2,
    )(info, offsets, *sum(snaps[:-1], []))
    outs = call(
        functools.partial(image_kernel, 1, False),
        "image_last",
        (struct(noffsets // groups, TILE, 8, LANES),) * groups,
        [SM, SM] + [VM] * 7,
        scratch=[pltpu.VMEM((1, *wide), F32)] * 2,
    )(info, offsets, partial[0], *snaps[-1])
    parts = [outs[0]] + [
        lax.ppermute(outs[d], "grp", [(i, i ^ d) for i in range(groups)]) for d in range(1, groups)
    ]
    return call(
        gather_kernel,
        "gather",
        struct(noffsets // groups, TILE, TILE, 2 * LANES),
        [SM] + [VM] * 4,
        scratch=[pltpu.VMEM((groups, noffsets // groups, TILE, 8, LANES), F32)],
    )(info, *parts)


def solution(mesh):
    return jax.shard_map(
        shards,
        mesh=mesh,
        in_specs=(
            P(None, None, None, "gx", "gy", None),
            P("gx", "gy", None),
            P("gx", "gy", None),
            P("gx", "gy", None),
            P(),
            P(),
            P(),
        ),
        out_specs=P("grp", "gx", "gy", None),
        check_vma=False,
    )
```

```python
import functools

import jax
import jax.numpy as jnp
from jax import lax
from jax.experimental import pallas as pl
from jax.experimental.pallas import tpu as pltpu
from jax.sharding import PartitionSpec as P

NSTEPS = 16
SNAP = 4
HMAX = 8
BLOCKS = NSTEPS // SNAP
NW = 2
LANES = 128
TILE = 16
EXT = TILE + 2 * SNAP
YPAD = 8
YROWS = EXT + 2 * YPAD
FIELDS = ((0, 4, 0), (1, 3, 4), (2, 3, 7), (3, 2, 10))
ROWS = 12
FROWS = NW * ROWS
CROWS = 9
GROUPED = 16
PARITY, LEFT, RIGHT, LOW, HIGH, START, FIRST, CHUNK, GROUP = range(9)

VM = pl.BlockSpec(memory_space=pltpu.VMEM)
SM = pl.BlockSpec(memory_space=pltpu.SMEM)
F32 = jnp.float32


def struct(*shape, dtype=F32):
    return jax.ShapeDtypeStruct(shape, dtype)


def call(kernel, name, outs, in_specs, scratch=(), out_specs=None, cost=2_000_000):
    return pl.pallas_call(
        kernel,
        out_shape=outs,
        in_specs=in_specs,
        out_specs=out_specs if out_specs is not None else jax.tree.map(lambda _: VM, outs),
        scratch_shapes=list(scratch),
        compiler_params=pltpu.CompilerParams(vmem_limit_bytes=40 << 20),
        cost_estimate=pl.CostEstimate(flops=cost, bytes_accessed=cost, transcendentals=0),
        name=name,
    )


def lane_iota(rows=8):
    return lax.broadcasted_iota(jnp.int32, (rows, LANES), 1)


def strips(info, state, width, rows, first, second):
    even = 1 - info[PARITY]
    far = TILE - width
    first[rows : rows + width] = state[pl.ds(even * far, width)]
    second[rows : rows + width] = state[pl.ds((1 - even) * far, width)]


def sides(info, first, second, row):
    odd = info[PARITY] == 1
    a, b = first[row], second[row]
    left = jnp.where(odd, a, b)
    right = jnp.where(odd, b, a)
    zero = jnp.zeros_like(a)
    return jnp.where(info[LEFT] == 1, left, zero), jnp.where(info[RIGHT] == 1, right, zero)


def prepare(info, check_in, courant_in, epsilon_in, delta_in, state, coef, s1, s2, *scratch):
    check, courant, epsilon, delta, sems = scratch
    copies = [
        pltpu.make_async_copy(source, target, sems.at[i])
        for i, (source, target) in enumerate(
            [(courant_in, courant), (epsilon_in, epsilon), (delta_in, delta), (check_in, check)]
        )
    ]
    for copy in copies:
        copy.start()
    start = info[START]
    shift = lax.rem(LANES - start, LANES)
    low = lane_iota(TILE) < LANES - start

    def window(block):
        return jnp.where(
            low,
            pltpu.roll(block[:, :LANES], shift, 1),
            pltpu.roll(block[:, LANES:], shift, 1),
        )

    for copy in copies[:3]:
        copy.wait()
    for x in range(TILE):
        c = window(courant[x])
        e = window(epsilon[x])
        d = window(delta[x])
        coef[0, x] = c + 2.0 * c * e
        coef[1, x] = c * jnp.sqrt(2.0 * d + 1.0)
        coef[2, x] = c
    for k in range(3):
        strips(info, coef.at[k], 3, FROWS + 3 * k, s1, s2)
    copies[3].wait()
    for w in range(NW):
        for f, width, row in FIELDS:
            for x in range(TILE):
                state[w, f, x] = window(check[w, f // 2, f % 2, x])
            strips(info, state.at[w, f], width, w * ROWS + row, s1, s2)


def listing(most, code, cells, points, count):
    for row in range(code.shape[0]):

        def some(group, n):
            def each(n):
                for i in range(GROUPED):
                    at = group * GROUPED + i
                    value = code[row, at]
                    cells[row, n] = value
                    points[row, n] = at
                    n = n + jnp.where(value >= 0, 1, 0)
                return n

            return lax.cond(most[row, group] >= 0, each, lambda n: n, n)

        count[row] = lax.fori_loop(0, code.shape[1] // GROUPED, some, jnp.int32(0))


def coef_whole(info, coef, r1, r2, below, above, out):
    stride = FROWS + CROWS
    out[...] = jnp.zeros_like(out)
    for k in range(3):
        out[k, SNAP : SNAP + TILE, SNAP : SNAP + TILE] = coef[k]
        for row in range(3):
            left, right = sides(info, r1, r2, FROWS + 3 * k + row)
            out[k, 1 + row, SNAP : SNAP + TILE] = left
            out[k, SNAP + TILE + row, SNAP : SNAP + TILE] = right
        for x in range(1, EXT - 1):
            at = x * stride + FROWS + 3 * k
            lo = below[at : at + 3]
            hi = above[at : at + 3]
            out[k, x, 1:4] = jnp.where(info[LOW] == 1, lo, jnp.zeros_like(lo))
            out[k, x, SNAP + TILE : SNAP + TILE + 3] = jnp.where(info[HIGH] == 1, hi, jnp.zeros_like(hi))


def edge_rows(info, *refs):
    state, *coef, r1, r2, low, high = refs
    stride = low.shape[0] // EXT
    arrays = [(state.at[w, f], width, w * ROWS + row) for w in range(NW) for f, width, row in FIELDS]
    arrays += [(coef[0].at[k], 3, FROWS + 3 * k) for k in range(3) if coef]
    for own, width, row in arrays:
        for n in range(width):
            left, right = sides(info, r1, r2, row + n)
            for x, layer in ((SNAP - width + n, left), (SNAP + TILE + n, right)):
                at = x * stride + row
                low[at : at + width] = layer[:width]
                high[at : at + width] = layer[TILE - width :]
        for x in range(TILE):
            at = (x + SNAP) * stride + row
            low[at : at + width] = own[x, :width]
            high[at : at + width] = own[x, TILE - width :]
        for x in [*range(SNAP - width), *range(EXT - SNAP + width, EXT)]:
            at = x * stride + row
            low[at : at + width] = jnp.zeros((width, LANES), F32)
            high[at : at + width] = jnp.zeros((width, LANES), F32)


def block_kernel(rows, has_state, last, joined, *refs):
    refs = list(refs)
    info, cells, points, count, amps, coef = refs[:6]
    refs = refs[6:]
    if has_state:
        state, r1, r2, below, above = refs[:5]
        refs = refs[5:]
        stride = below.shape[0] // EXT
    if joined:
        beside, refs = refs[0], refs[1:]
    if not last:
        out_state, refs = refs[0], refs[1:]
    if last and not joined:
        snap, refs = refs[0], refs[1:]
    else:
        snap, s1, s2 = refs[:3]
        refs = refs[3:]
    bufs = refs
    own = slice(YPAD + SNAP, YPAD + SNAP + TILE)
    if has_state:
        for w in range(NW):
            for f, width, row in FIELDS:
                at = w * ROWS + row
                bufs[f][w, SNAP : SNAP + TILE, own] = state[w, f]
                for n in range(width):
                    left, right = sides(info, r1, r2, at + n)
                    bufs[f][w, SNAP - width + n, own] = left
                    bufs[f][w, SNAP + TILE + n, own] = right
                for x in range(SNAP - width, SNAP + TILE + width):
                    lo = below[x * stride + at : x * stride + at + width]
                    hi = above[x * stride + at : x * stride + at + width]
                    bufs[f][w, x, YPAD + SNAP - width : YPAD + SNAP] = jnp.where(
                        info[LOW] == 1, lo, jnp.zeros_like(lo)
                    )
                    bufs[f][w, x, YPAD + SNAP + TILE : YPAD + SNAP + TILE + width] = jnp.where(
                        info[HIGH] == 1, hi, jnp.zeros_like(hi)
                    )
    else:
        for buf in bufs:
            buf[...] = jnp.zeros_like(buf)

    lanes = lane_iota()
    bottom, top = lanes == 0, lanes == LANES - 1
    one_row = lane_iota(1)
    for step in range(SNAP):
        extent = SNAP - 1 - step
        now, then = (bufs[:2], bufs[2:]) if step % 2 == 0 else (bufs[2:], bufs[:2])
        main, aux = now
        main_next, aux_next = then

        def layer(x):
            for chunk in range(EXT // 8):
                at = YPAD + 8 * chunk
                mid = pl.ds(at, 8)
                horizontal = coef[0, x, 8 * chunk : 8 * chunk + 8]
                coupling = coef[1, x, 8 * chunk : 8 * chunk + 8]
                vertical = coef[2, x, 8 * chunk : 8 * chunk + 8]
                for w in range(NW):
                    m = main[w, x, mid]
                    across = (
                        (main[w, x + 1, mid] + main[w, x - 1, mid])
                        + (main[w, x, pl.ds(at + 1, 8)] + main[w, x, pl.ds(at - 1, 8)])
                        - 4.0 * m
                    )
                    a = aux[w, x, mid]
                    deeper = jnp.where(top, 0.0, pltpu.roll(a, LANES - 1, 1))
                    upper = jnp.where(bottom, 0.0, pltpu.roll(a, 1, 1))
                    down = deeper + upper - 2.0 * a
                    main_next[w, x, mid] = (
                        2.0 * m - main_next[w, x, mid] + (horizontal * across + coupling * down)
                    )
                    aux_next[w, x, mid] = (
                        2.0 * a - aux_next[w, x, mid] + (coupling * across + vertical * down)
                    )

        for x in range(SNAP - extent, SNAP + TILE + extent):
            layer(x)
        for w in range(NW):

            def inject(i, carry):
                cell = cells[rows[w], i]
                amount = amps[w, step, points[rows[w], i]]
                x = lax.shift_right_logical(cell, 16)
                y = lax.bitwise_and(lax.shift_right_logical(cell, 8), 255)
                z = lax.bitwise_and(cell, 255)
                add = jnp.where(one_row == z, amount, 0.0)
                main_next[w, x, pl.ds(y, 1)] += add
                aux_next[w, x, pl.ds(y, 1)] += add
                return carry

            lax.fori_loop(0, count[rows[w]], inject, 0)

    for x in range(TILE):
        snap[x] = packed(info, bufs[0][0, x + SNAP, own], bufs[0][1, x + SNAP, own])
    if not last:
        for w in range(NW):
            for f, width, row in FIELDS:
                out_state[w, f] = bufs[f][w, SNAP : SNAP + TILE, own]
                strips(info, out_state.at[w, f], width, w * ROWS + row, s1, s2)
        even = 1 - info[PARITY]
        s1[FROWS:] = snap[pl.ds(SNAP + SNAP * even, HMAX - SNAP)]
        s2[FROWS:] = snap[pl.ds(SNAP + SNAP * (1 - even), HMAX - SNAP)]
    elif joined:
        strips(info, snap, HMAX, 0, s1, s2)
        strips(info, beside, HMAX, HMAX, s1, s2)


def packed(info, first, second):
    to_left = lax.rem(LANES - info[FIRST], LANES)
    to_right = lax.rem(LANES + LANES // 2 - info[FIRST], LANES)
    return jnp.where(
        lane_iota(TILE) < LANES // 2, pltpu.roll(first, to_left, 1), pltpu.roll(second, to_right, 1)
    )


def widen_far(info, own, r1, r2, base, out):
    out[HMAX : HMAX + TILE] = own[...]
    for row in range(HMAX):
        left, right = sides(info, r1, r2, base + row)
        out[row] = left
        out[HMAX + TILE + row] = right


def widen(info, own, r1, r2, out):
    out[HMAX : HMAX + TILE] = own[...]
    for row in range(SNAP):
        left, right = sides(info, r1, r2, FROWS + row)
        out[row] = left
        out[HMAX + TILE + SNAP + row] = right
        ends = [sides(info, r1, r2, w * ROWS + row) for w in range(NW)]
        out[SNAP + row] = packed(info, ends[0][0], ends[1][0])
        out[HMAX + TILE + row] = packed(info, ends[0][1], ends[1][1])


def image_kernel(count, first, *refs):
    refs = list(refs)
    info, offsets = refs[:2]
    refs = refs[2:]
    if not first:
        before, refs = refs[0], refs[1:]
    if first:
        snaps, refs = refs[: 6 * count], refs[6 * count :]
    else:
        (own_source, own_receiver, r1, r2), refs = refs[:4], refs[4:]
    outs, (source, receiver) = refs[:-2], refs[-2:]
    if first:
        for j in range(count):
            widen(info, *snaps[6 * j : 6 * j + 3], source.at[j])
            widen(info, *snaps[6 * j + 3 : 6 * j + 6], receiver.at[j])
    else:
        widen_far(info, own_source, r1, r2, 0, source.at[0])
        widen_far(info, own_receiver, r1, r2, HMAX, receiver.at[0])
    half = lax.broadcasted_iota(jnp.int32, (TILE, 8, LANES), 2) < LANES // 2
    group = info[GROUP]
    for d in range(4):
        for i in range(4):
            shift = offsets[4 * lax.bitwise_xor(group, d) + i]

            at_source = pl.ds(HMAX - shift, TILE)
            at_receiver = pl.ds(HMAX + shift, TILE)
            sums = []
            for y in range(2):
                rows = slice(8 * y, 8 * y + 8)
                total = source[0, at_source, rows] * receiver[0, at_receiver, rows]
                for j in range(1, count):
                    total += source[j, at_source, rows] * receiver[j, at_receiver, rows]
                if not first:
                    total += before[4 * d + i, :, rows]
                sums.append(total)
            if first:
                for y in range(2):
                    outs[0][4 * d + i, :, 8 * y : 8 * y + 8] = sums[y]
            else:
                a, b = (t + pltpu.roll(t, LANES // 2, 2) for t in sums)
                outs[d][i] = jnp.where(half, a, b)


def gather_kernel(info, *refs):
    parts, out, held = refs[:4], refs[4], refs[5]
    for d in range(4):
        held[d] = parts[d][...]
    half = lax.broadcasted_iota(jnp.int32, (TILE, 8, LANES), 2) < LANES // 2
    mine = info[CHUNK]
    for tile in range(2):
        low = lax.bitwise_xor(mine, 2 * tile)
        high = lax.bitwise_xor(mine, 2 * tile + 1)
        at = slice(tile * LANES, (tile + 1) * LANES)
        for i in range(4):
            a = held[low, i]
            b = held[high, i]
            out[i, :, 0:8, at] = jnp.where(half, a, pltpu.roll(b, LANES // 2, 2))
            out[i, :, 8:16, at] = jnp.where(half, pltpu.roll(a, LANES // 2, 2), b)


def shards(checkpoint, courant, epsilon, delta, positions, amplitudes, offsets):
    group, gx, gy = (lax.axis_index(axis) for axis in ("grp", "gx", "gy"))
    groups, nx, ny = (lax.axis_size(axis) for axis in ("grp", "gx", "gy"))
    quarter = courant.shape[2] // groups
    chunk = group
    start = jnp.clip(quarter * chunk - quarter // 2, 0, courant.shape[2] - LANES)
    info = jnp.stack(
        [
            gx % 2,
            (gx > 0).astype(jnp.int32),
            (gx < nx - 1).astype(jnp.int32),
            (gy > 0).astype(jnp.int32),
            (gy < ny - 1).astype(jnp.int32),
            start,
            quarter * chunk - start,
            chunk,
            group,
        ]
    ).astype(jnp.int32)

    pair = [(i, i ^ 1) for i in range(nx)]
    other = [(i, ((i - 1) % nx ^ 1) + 1) for i in range(nx)]
    other = [(i, j % nx) for i, j in other]

    def swap_x(first, second):
        return lax.ppermute(first, "gx", pair), lax.ppermute(second, "gx", other)

    def swap_y(low, high):
        below = lax.ppermute(high, "gy", [(i, (i + 1) % ny) for i in range(ny)])
        above = lax.ppermute(low, "gy", [(i, (i - 1) % ny) for i in range(ny)])
        return below, above

    local_x = positions[:, 0] - gx * TILE + SNAP
    local_y = positions[:, 1] - gy * TILE + SNAP
    local_z = positions[:, 2] - start
    inside = (local_x >= 1) & (local_x < EXT - 1) & (local_y >= 1) & (local_y < EXT - 1)
    inside &= (local_z >= 0) & (local_z < LANES)
    code = jnp.where(inside, (local_x << 16) | ((local_y + YPAD) << 8) | local_z, -1)
    rows, npoints = code.shape
    lists = call(
        listing,
        "listing",
        (
            struct(rows, npoints, dtype=jnp.int32),
            struct(rows, npoints, dtype=jnp.int32),
            struct(rows, dtype=jnp.int32),
        ),
        [SM, SM],
        out_specs=(SM, SM, SM),
    )(code.reshape(rows, npoints // GROUPED, GROUPED).max(axis=2), code)

    state, coef, s1, s2 = call(
        prepare,
        "prepare",
        (
            struct(NW, 4, TILE, TILE, LANES),
            struct(3, TILE, TILE, LANES),
            struct(FROWS + CROWS, TILE, LANES),
            struct(FROWS + CROWS, TILE, LANES),
        ),
        [SM] + [pl.BlockSpec(memory_space=pl.ANY)] * 4,
        scratch=[pltpu.VMEM(a.shape, F32) for a in (checkpoint, courant, epsilon, delta)]
        + [pltpu.SemaphoreType.DMA((4,))],
    )(info, checkpoint, courant, epsilon, delta)

    def exchange(arrays, s1, s2):
        r1, r2 = swap_x(s1, s2)
        rows = (FROWS + CROWS if len(arrays) > 1 else FROWS) * EXT
        low, high = call(
            edge_rows,
            "edge_rows",
            (struct(rows, LANES), struct(rows, LANES)),
            [SM] + [VM] * (2 + len(arrays)),
        )(info, *arrays, r1, r2)
        return (r1, r2, *swap_y(low, high))

    halo = exchange((state, coef), s1, s2)
    coef = call(coef_whole, "coef_whole", struct(3, EXT, EXT, LANES), [SM] + [VM] * 5)(
        info, coef, *halo
    )

    def run_block(number, chain, halo, beside=()):
        last = number == BLOCKS - 1
        amps = amplitudes[chain::2, number * SNAP : (number + 1) * SNAP]
        outs = [struct(TILE, TILE, LANES)]
        if not last:
            strip = struct(FROWS + HMAX - SNAP, TILE, LANES)
            outs = [struct(NW, 4, TILE, TILE, LANES), *outs, strip, strip]
        elif beside:
            outs += [struct(2 * HMAX, TILE, LANES)] * 2
        return call(
            functools.partial(
                block_kernel, (chain, chain + 2), bool(halo), last, bool(beside)
            ),
            "block",
            tuple(outs),
            [SM] * 5 + [VM] * (1 + len(halo) + len(beside)),
            scratch=[pltpu.VMEM((NW, EXT, YROWS, LANES), F32)] * 4,
            cost=8_000_000,
        )(info, *lists, amps, coef, *halo, *beside)

    snaps = []
    halos = [(state, *halo), ()]
    for number in range(BLOCKS - 1):
        pieces = []
        for chain in (1, 0):
            state, snap, s1, s2 = run_block(number, chain, halos[chain])
            strips_back = exchange((state,), s1, s2)
            halos[chain] = (state, *strips_back)
            pieces = [snap, *strips_back[:2]] + pieces
        snaps += pieces

    (receiver,) = run_block(BLOCKS - 1, 1, halos[1])
    source, s1, s2 = run_block(BLOCKS - 1, 0, halos[0], (receiver,))
    final = [source, receiver, *swap_x(s1, s2)]

    noffsets = offsets.shape[0]
    wide = [TILE + 2 * HMAX, TILE, LANES]
    partial = call(
        functools.partial(image_kernel, BLOCKS - 1, True),
        "image",
        (struct(noffsets, TILE, TILE, LANES),),
        [SM, SM] + [VM] * (6 * (BLOCKS - 1)),
        scratch=[pltpu.VMEM((BLOCKS - 1, *wide), F32)] * 2,
    )(info, offsets, *snaps)
    outs = call(
        functools.partial(image_kernel, 1, False),
        "image_last",
        (struct(noffsets // groups, TILE, 8, LANES),) * groups,
        [SM, SM] + [VM] * 5,
        scratch=[pltpu.VMEM((1, *wide), F32)] * 2,
    )(info, offsets, partial[0], *final)
    parts = [outs[0]] + [
        lax.ppermute(outs[d], "grp", [(i, i ^ d) for i in range(groups)]) for d in range(1, groups)
    ]
    return call(
        gather_kernel,
        "gather",
        struct(noffsets // groups, TILE, TILE, 2 * LANES),
        [SM] + [VM] * 4,
        scratch=[pltpu.VMEM((groups, noffsets // groups, TILE, 8, LANES), F32)],
    )(info, *parts)


def solution(mesh):
    return jax.shard_map(
        shards,
        mesh=mesh,
        in_specs=(
            P(None, None, None, "gx", "gy", None),
            P("gx", "gy", None),
            P("gx", "gy", None),
            P("gx", "gy", None),
            P(),
            P(),
            P(),
        ),
        out_specs=P("grp", "gx", "gy", None),
        check_vma=False,
    )
```

```python
import functools

import jax
import jax.numpy as jnp
from jax import lax
from jax.experimental import pallas as pl
from jax.experimental.pallas import tpu as pltpu
from jax.sharding import PartitionSpec as P

NSTEPS = 16
SNAP = 4
MIRROR = True
HMAX = 8
BLOCKS = NSTEPS // SNAP
NW = 2
LANES = 128
TILE = 16
EXT = TILE + 2 * SNAP
YPAD = 8
YROWS = EXT + 2 * YPAD
FIELDS = ((0, 4, 0), (1, 3, 4), (2, 3, 7), (3, 2, 10))
ROWS = 12
FROWS = NW * ROWS
CROWS = 9
XROWS = 3 * FROWS // 4
GROUPED = 16
PARITY, LEFT, RIGHT, LOW, HIGH, START, FIRST, CHUNK, GROUP, BASE = range(10)
SENT = 3 * LANES // 4

VM = pl.BlockSpec(memory_space=pltpu.VMEM)
SM = pl.BlockSpec(memory_space=pltpu.SMEM)
F32 = jnp.float32


def struct(*shape, dtype=F32):
    return jax.ShapeDtypeStruct(shape, dtype)


def call(kernel, name, outs, in_specs, scratch=(), out_specs=None, cost=2_000_000, after=()):
    run = pl.pallas_call(
        lambda *refs: kernel(*refs[len(after) :]),
        out_shape=outs,
        in_specs=[pl.BlockSpec(memory_space=pl.ANY)] * len(after) + in_specs,
        out_specs=out_specs if out_specs is not None else jax.tree.map(lambda _: VM, outs),
        scratch_shapes=list(scratch),
        compiler_params=pltpu.CompilerParams(vmem_limit_bytes=40 << 20),
        cost_estimate=pl.CostEstimate(flops=cost, bytes_accessed=cost, transcendentals=0),
        name=name,
    )
    return functools.partial(run, *after)


def lane_iota(rows=8):
    return lax.broadcasted_iota(jnp.int32, (rows, LANES), 1)


def strips(info, state, width, rows, first, second):
    even = 1 - info[PARITY]
    far = TILE - width
    first[rows : rows + width] = state[pl.ds(even * far, width)]
    second[rows : rows + width] = state[pl.ds((1 - even) * far, width)]


def sides(info, first, second, row, whole=True):
    odd = info[PARITY] == 1
    if whole:
        a, b = first[row], second[row]
    else:
        a, b = unpacked(info, first, FROWS, row), unpacked(info, second, FROWS, row)
    left = jnp.where(odd, a, b)
    right = jnp.where(odd, b, a)
    zero = jnp.zeros_like(a)
    return jnp.where(info[LEFT] == 1, left, zero), jnp.where(info[RIGHT] == 1, right, zero)


def turned(info, block, by):
    return pltpu.roll(block, lax.rem(2 * LANES + by, LANES), block.ndim - 1)


def pack(info, source, out):
    n = source.shape[0] // 4
    wide = lax.broadcasted_iota(jnp.int32, (source.shape[1], LANES), 1) < SENT
    base = info[BASE]
    for i in range(n):
        for part in range(3):
            out[part * n + i] = jnp.where(
                wide,
                turned(info, source[part * n + i], -base),
                turned(info, source[3 * n + i], SENT - (LANES - SENT) * part - base),
            )


def unpacked(info, source, count, at):
    n = count // 4
    base = info[BASE]
    if at < 3 * n:
        return turned(info, source[at], base)
    rows = [source[part * n + at - 3 * n] for part in range(3)]
    lanes = lax.broadcasted_iota(jnp.int32, rows[0].shape, 1) - base
    step = LANES - SENT
    a, b, c = (turned(info, row, base - SENT + step * part) for part, row in enumerate(rows))
    return jnp.where(lanes < step, a, jnp.where(lanes < 2 * step, b, c))


def fetch(pairs, sems):
    copies = [
        pltpu.make_async_copy(source, target, sems.at[i]) for i, (source, target) in enumerate(pairs)
    ]
    for copy in copies:
        copy.start()
    for copy in copies:
        copy.wait()


def window(info, block):
    start = info[START]
    shift = lax.rem(LANES - start, LANES)
    return jnp.where(
        lane_iota(TILE) < LANES - start,
        pltpu.roll(block[:, :LANES], shift, 1),
        pltpu.roll(block[:, LANES:], shift, 1),
    )


def prepare_coef(info, courant_in, epsilon_in, delta_in, coef, c1, c2, courant, epsilon, delta, sems):
    fetch([(courant_in, courant), (epsilon_in, epsilon), (delta_in, delta)], sems)
    for x in range(TILE):
        c = window(info, courant[x])
        e = window(info, epsilon[x])
        d = window(info, delta[x])
        coef[0, x] = c + 2.0 * c * e
        coef[1, x] = c * jnp.sqrt(2.0 * d + 1.0)
        coef[2, x] = c
    for k in range(3):
        strips(info, coef.at[k], 3, 3 * k, c1, c2)


def prepare_state(info, check_in, state, s1, s2, check, sems, lay1, lay2):
    fetch([(check_in.at[w], check.at[w]) for w in range(NW)], sems)
    for w in range(NW):
        for f, width, row in FIELDS:
            for x in range(TILE):
                state[w, f, x] = window(info, check[w, f // 2, f % 2, x])
            strips(info, state.at[w, f], width, w * ROWS + row, lay1, lay2)
    pack(info, lay1, s1)
    pack(info, lay2, s2)


def listing(most, code, cells, points, count):
    for row in range(code.shape[0]):

        def some(group, n):
            def each(n):
                for i in range(GROUPED):
                    at = group * GROUPED + i
                    value = code[row, at]
                    cells[row, n] = value
                    points[row, n] = at
                    n = n + jnp.where(value >= 0, 1, 0)
                return n

            return lax.cond(most[row, group] >= 0, each, lambda n: n, n)

        count[row] = lax.fori_loop(0, code.shape[1] // GROUPED, some, jnp.int32(0))


def coef_whole(info, coef, r1, r2, below, above, out):
    out[...] = jnp.zeros_like(out)
    for k in range(3):
        out[k, SNAP : SNAP + TILE, SNAP : SNAP + TILE] = coef[k]
        for row in range(3):
            left, right = sides(info, r1, r2, 3 * k + row)
            out[k, 1 + row, SNAP : SNAP + TILE] = left
            out[k, SNAP + TILE + row, SNAP : SNAP + TILE] = right
        for x in range(1, EXT - 1):
            at = x * CROWS + 3 * k
            lo = below[at : at + 3]
            hi = above[at : at + 3]
            out[k, x, 1:4] = jnp.where(info[LOW] == 1, lo, jnp.zeros_like(lo))
            out[k, x, SNAP + TILE : SNAP + TILE + 3] = jnp.where(info[HIGH] == 1, hi, jnp.zeros_like(hi))


def field_rows(info, state, r1, r2, low, high, low_rows, high_rows):
    own = [(state.at[w, f], width, w * ROWS + row) for w in range(NW) for f, width, row in FIELDS]
    edge_rows(info, own, FROWS, False, r1, r2, low_rows, high_rows)
    for rows, out in ((low_rows, low), (high_rows, high)):
        pack(info, rows.reshape(EXT * FROWS // 8, 8, LANES), out)


def coef_rows(info, coef, r1, r2, low, high):
    edge_rows(info, [(coef.at[k], 3, 3 * k) for k in range(3)], CROWS, True, r1, r2, low, high)


def edge_rows(info, arrays, stride, whole, r1, r2, low, high):
    for own, width, row in arrays:
        for n in range(width):
            left, right = sides(info, r1, r2, row + n, whole)
            for x, layer in ((SNAP - width + n, left), (SNAP + TILE + n, right)):
                at = x * stride + row
                low[at : at + width] = layer[:width]
                high[at : at + width] = layer[TILE - width :]
        for x in range(TILE):
            at = (x + SNAP) * stride + row
            low[at : at + width] = own[x, :width]
            high[at : at + width] = own[x, TILE - width :]
        for x in [*range(SNAP - width), *range(EXT - SNAP + width, EXT)]:
            at = x * stride + row
            low[at : at + width] = jnp.zeros((width, LANES), F32)
            high[at : at + width] = jnp.zeros((width, LANES), F32)


def block_kernel(rows, has_state, last, joined, *refs):
    refs = list(refs)
    info, cells, points, count, amps, coef = refs[:6]
    refs = refs[6:]
    if has_state:
        state, r1, r2, below, above = refs[:5]
        refs = refs[5:]
    if joined:
        beside, refs = refs[0], refs[1:]
    if not last:
        out_state, refs = refs[0], refs[1:]
    if last and not joined:
        snap, refs = refs[0], refs[1:]
    else:
        snap, s1, s2 = refs[:3]
        refs = refs[3:]
    bufs = refs[:4]
    lay1, lay2, below_rows, above_rows = refs[4:]
    own = slice(YPAD + SNAP, YPAD + SNAP + TILE)
    if has_state:
        for rows_in, rows_out in ((below, below_rows), (above, above_rows)):
            for i in range(EXT * FROWS // 8):
                rows_out[8 * i : 8 * i + 8] = unpacked(info, rows_in, EXT * FROWS // 8, i)
        for w in range(NW):
            for f, width, row in FIELDS:
                at = w * ROWS + row
                bufs[f][w, SNAP : SNAP + TILE, own] = state[w, f]
                for n in range(width):
                    left, right = sides(info, r1, r2, at + n, False)
                    bufs[f][w, SNAP - width + n, own] = left
                    bufs[f][w, SNAP + TILE + n, own] = right
                for x in range(SNAP - width, SNAP + TILE + width):
                    lo = below_rows[x * FROWS + at : x * FROWS + at + width]
                    hi = above_rows[x * FROWS + at : x * FROWS + at + width]
                    bufs[f][w, x, YPAD + SNAP - width : YPAD + SNAP] = jnp.where(
                        info[LOW] == 1, lo, jnp.zeros_like(lo)
                    )
                    bufs[f][w, x, YPAD + SNAP + TILE : YPAD + SNAP + TILE + width] = jnp.where(
                        info[HIGH] == 1, hi, jnp.zeros_like(hi)
                    )
    else:
        for buf in bufs:
            buf[...] = jnp.zeros_like(buf)

    lanes = lane_iota()
    bottom, top = lanes == 0, lanes == LANES - 1
    one_row = lane_iota(1)
    for step in range(SNAP):
        extent = SNAP - 1 - step
        now, then = (bufs[:2], bufs[2:]) if step % 2 == 0 else (bufs[2:], bufs[:2])
        main, aux = now
        main_next, aux_next = then

        def layer(x):
            for chunk in range(EXT // 8):
                at = YPAD + 8 * chunk
                mid = pl.ds(at, 8)
                horizontal = coef[0, x, 8 * chunk : 8 * chunk + 8]
                coupling = coef[1, x, 8 * chunk : 8 * chunk + 8]
                vertical = coef[2, x, 8 * chunk : 8 * chunk + 8]
                for w in range(NW):
                    m = main[w, x, mid]
                    across = (
                        (main[w, x + 1, mid] + main[w, x - 1, mid])
                        + (main[w, x, pl.ds(at + 1, 8)] + main[w, x, pl.ds(at - 1, 8)])
                        - 4.0 * m
                    )
                    a = aux[w, x, mid]
                    deeper = jnp.where(top, 0.0, pltpu.roll(a, LANES - 1, 1))
                    upper = jnp.where(bottom, 0.0, pltpu.roll(a, 1, 1))
                    down = deeper + upper - 2.0 * a
                    main_next[w, x, mid] = (
                        2.0 * m - main_next[w, x, mid] + (horizontal * across + coupling * down)
                    )
                    aux_next[w, x, mid] = (
                        2.0 * a - aux_next[w, x, mid] + (coupling * across + vertical * down)
                    )

        for x in range(SNAP - extent, SNAP + TILE + extent):
            layer(x)
        for w in range(NW):

            def inject(i, carry):
                cell = cells[rows[w], i]
                amount = amps[w, step, points[rows[w], i]]
                x = lax.shift_right_logical(cell, 16)
                y = lax.bitwise_and(lax.shift_right_logical(cell, 8), 255)
                z = lax.bitwise_and(cell, 255)
                add = jnp.where(one_row == z, amount, 0.0)
                main_next[w, x, pl.ds(y, 1)] += add
                aux_next[w, x, pl.ds(y, 1)] += add
                return carry

            lax.fori_loop(0, count[rows[w]], inject, 0)

    for x in range(TILE):
        snap[x] = packed(info, bufs[0][0, x + SNAP, own], bufs[0][1, x + SNAP, own])
    if not last:
        for w in range(NW):
            for f, width, row in FIELDS:
                out_state[w, f] = bufs[f][w, SNAP : SNAP + TILE, own]
                strips(info, out_state.at[w, f], width, w * ROWS + row, lay1, lay2)
        pack(info, lay1, s1)
        pack(info, lay2, s2)
        even = 1 - info[PARITY]
        s1[XROWS:] = snap[pl.ds(SNAP + SNAP * even, HMAX - SNAP)]
        s2[XROWS:] = snap[pl.ds(SNAP + SNAP * (1 - even), HMAX - SNAP)]
    elif joined:
        strips(info, snap, HMAX, 0, s1, s2)
        strips(info, beside, HMAX, HMAX, s1, s2)


def packed(info, first, second):
    to_left = lax.rem(LANES - info[FIRST], LANES)
    to_right = lax.rem(LANES + LANES // 2 - info[FIRST], LANES)
    return jnp.where(
        lane_iota(TILE) < LANES // 2, pltpu.roll(first, to_left, 1), pltpu.roll(second, to_right, 1)
    )


def widen_far(info, own, r1, r2, base, out):
    out[HMAX : HMAX + TILE] = own[...]
    for row in range(HMAX):
        left, right = sides(info, r1, r2, base + row)
        out[row] = left
        out[HMAX + TILE + row] = right


def widen(info, own, r1, r2, out):
    out[HMAX : HMAX + TILE] = own[...]
    for row in range(SNAP):
        left, right = sides(info, r1, r2, XROWS + row)
        out[row] = left
        out[HMAX + TILE + SNAP + row] = right
        ends = [sides(info, r1, r2, w * ROWS + row, False) for w in range(NW)]
        out[SNAP + row] = packed(info, ends[0][0], ends[1][0])
        out[HMAX + TILE + row] = packed(info, ends[0][1], ends[1][1])


def image_kernel(count, first, *refs):
    refs = list(refs)
    info, offsets = refs[:2]
    refs = refs[2:]
    if not first:
        before, refs = refs[0], refs[1:]
    if first:
        snaps, refs = refs[: 6 * count], refs[6 * count :]
    else:
        (own_source, own_receiver, r1, r2), refs = refs[:4], refs[4:]
    outs, (source, receiver) = refs[:-2], refs[-2:]
    if first:
        for j in range(count):
            widen(info, *snaps[6 * j : 6 * j + 3], source.at[j])
            widen(info, *snaps[6 * j + 3 : 6 * j + 6], receiver.at[j])
    else:
        widen_far(info, own_source, r1, r2, 0, source.at[0])
        widen_far(info, own_receiver, r1, r2, HMAX, receiver.at[0])
    half = lax.broadcasted_iota(jnp.int32, (TILE, 8, LANES), 2) < LANES // 2
    group = info[GROUP]
    for d in range(4):
        for i in range(4):
            shift = offsets[4 * lax.bitwise_xor(group, d) + i]

            at_source = pl.ds(HMAX - shift, TILE)
            at_receiver = pl.ds(HMAX + shift, TILE)
            sums = []
            for y in range(2):
                rows = slice(8 * y, 8 * y + 8)
                total = source[0, at_source, rows] * receiver[0, at_receiver, rows]
                for j in range(1, count):
                    total += source[j, at_source, rows] * receiver[j, at_receiver, rows]
                if not first:
                    total += before[4 * d + i, :, rows]
                sums.append(total)
            if first:
                for y in range(2):
                    outs[0][4 * d + i, :, 8 * y : 8 * y + 8] = sums[y]
            else:
                a, b = (t + pltpu.roll(t, LANES // 2, 2) for t in sums)
                outs[d][i] = jnp.where(half, a, b)


def gather_kernel(info, *refs):
    parts, out, held = refs[:4], refs[4], refs[5]
    for d in range(4):
        held[d] = parts[d][...]
    half = lax.broadcasted_iota(jnp.int32, (TILE, 8, LANES), 2) < LANES // 2
    mine = info[CHUNK]
    for tile in range(2):
        low = lax.bitwise_xor(mine, 2 * tile)
        high = lax.bitwise_xor(mine, 2 * tile + 1)
        at = slice(tile * LANES, (tile + 1) * LANES)
        for i in range(4):
            a = held[low, i]
            b = held[high, i]
            out[i, :, 0:8, at] = jnp.where(half, a, pltpu.roll(b, LANES // 2, 2))
            out[i, :, 8:16, at] = jnp.where(half, pltpu.roll(a, LANES // 2, 2), b)


def shards(checkpoint, courant, epsilon, delta, positions, amplitudes, offsets):
    group, gx, gy = (lax.axis_index(axis) for axis in ("grp", "gx", "gy"))
    groups, nx, ny = (lax.axis_size(axis) for axis in ("grp", "gx", "gy"))
    quarter = courant.shape[2] // groups
    far = (gx // 2) % 2
    chunk = jnp.where(far == 1, groups - 1 - group, group) if MIRROR else group
    start = jnp.clip(quarter * chunk - quarter // 2, 0, courant.shape[2] - LANES)
    info = jnp.stack(
        [
            gx % 2,
            (gx > 0).astype(jnp.int32),
            (gx < nx - 1).astype(jnp.int32),
            (gy > 0).astype(jnp.int32),
            (gy < ny - 1).astype(jnp.int32),
            start,
            quarter * chunk - start,
            chunk,
            group,
            (quarter * chunk - start) // 2,
        ]
    ).astype(jnp.int32)

    pair = [(i, i ^ 1) for i in range(nx)]
    other = [(i, ((i - 1) % nx ^ 1) + 1) for i in range(nx)]
    other = [(i, j % nx) for i, j in other]

    mirrored = [
        (g * nx + i, (groups - 1 - g) * nx + j) for g in range(groups) for i, j in other
    ]

    def swap_x(first, second):
        back = lax.ppermute(first, "gx", pair)
        if MIRROR:
            return back, lax.ppermute(second, ("grp", "gx"), mirrored)
        return back, lax.ppermute(second, "gx", other)

    def swap_y(low, high):
        below = lax.ppermute(high, "gy", [(i, (i + 1) % ny) for i in range(ny)])
        above = lax.ppermute(low, "gy", [(i, (i - 1) % ny) for i in range(ny)])
        return below, above

    local_x = positions[:, 0] - gx * TILE + SNAP
    local_y = positions[:, 1] - gy * TILE + SNAP
    local_z = positions[:, 2] - start
    inside = (local_x >= 1) & (local_x < EXT - 1) & (local_y >= 1) & (local_y < EXT - 1)
    inside &= (local_z >= 0) & (local_z < LANES)
    code = jnp.where(inside, (local_x << 16) | ((local_y + YPAD) << 8) | local_z, -1)
    rows, npoints = code.shape
    lists = call(
        listing,
        "listing",
        (
            struct(rows, npoints, dtype=jnp.int32),
            struct(rows, npoints, dtype=jnp.int32),
            struct(rows, dtype=jnp.int32),
        ),
        [SM, SM],
        out_specs=(SM, SM, SM),
    )(code.reshape(rows, npoints // GROUPED, GROUPED).max(axis=2), code)

    layers = [pltpu.VMEM((FROWS, TILE, LANES), F32)] * 2
    rows_whole = [pltpu.VMEM((EXT * FROWS, LANES), F32)] * 2
    rows_sent = struct(3 * EXT * FROWS // 32, 8, LANES)
    hbm = pl.BlockSpec(memory_space=pltpu.HBM)
    coef, c1, c2 = call(
        prepare_coef,
        "prepare_coef",
        (struct(3, TILE, TILE, LANES), struct(CROWS, TILE, LANES), struct(CROWS, TILE, LANES)),
        [SM] + [hbm] * 3,
        scratch=[pltpu.VMEM(courant.shape, F32)] * 3 + [pltpu.SemaphoreType.DMA((3,))],
    )(info, courant, epsilon, delta)
    ready = (c1,)
    c1, c2 = swap_x(c1, c2)
    state, s1, s2 = call(
        prepare_state,
        "prepare_state",
        (
            struct(NW, 4, TILE, TILE, LANES),
            struct(XROWS, TILE, LANES),
            struct(XROWS, TILE, LANES),
        ),
        [SM, hbm],
        scratch=[pltpu.VMEM(checkpoint.shape, F32), pltpu.SemaphoreType.DMA((NW,))] + layers,
        after=ready,
    )(info, checkpoint)
    s1, s2, _ = lax.optimization_barrier((s1, s2, c2))
    r1, r2 = swap_x(s1, s2)

    def rows_of(own, r1, r2, after=()):
        return call(
            field_rows,
            "field_rows",
            (rows_sent, rows_sent),
            [SM] + [VM] * 3,
            scratch=rows_whole,
            after=after,
        )(info, own, r1, r2)

    coef_edge = call(
        coef_rows,
        "coef_rows",
        (struct(CROWS * EXT, LANES),) * 2,
        [SM] + [VM] * 3,
    )(info, coef, c1, c2)
    below, above = swap_y(*coef_edge)
    edge = rows_of(state, r1, r2, after=coef_edge[:1])
    halo = (state, r1, r2, *swap_y(*edge))
    coef = call(coef_whole, "coef_whole", struct(3, EXT, EXT, LANES), [SM] + [VM] * 5)(
        info, coef, c1, c2, below, above
    )

    def run_block(number, chain, halo, beside=(), after=()):
        last = number == BLOCKS - 1
        amps = amplitudes[chain::2, number * SNAP : (number + 1) * SNAP]
        outs = [struct(TILE, TILE, LANES)]
        if not last:
            strip = struct(XROWS + HMAX - SNAP, TILE, LANES)
            outs = [struct(NW, 4, TILE, TILE, LANES), *outs, strip, strip]
        elif beside:
            outs += [struct(2 * HMAX, TILE, LANES)] * 2
        return call(
            functools.partial(
                block_kernel, (chain, chain + 2), bool(halo), last, bool(beside)
            ),
            "block",
            tuple(outs),
            [SM] * 5 + [VM] * (1 + len(halo) + len(beside)),
            scratch=[pltpu.VMEM((NW, EXT, YROWS, LANES), F32)] * 4 + layers + rows_whole,
            cost=8_000_000,
            after=after,
        )(info, *lists, amps, coef, *halo, *beside)

    snaps = []
    back = run_block(0, 1, ())
    for number in range(BLOCKS - 1):
        state_r, snap_r, *strips_r = back
        r1, r2 = swap_x(*strips_r)
        edge_r = rows_of(state_r, r1, r2, after=edge[:1])
        halo_r = (state_r, r1, r2, *swap_y(*edge_r))
        state, snap, *strips_s = run_block(number, 0, halo, after=edge_r[:1])
        q1, q2 = swap_x(*strips_s)
        back = run_block(number + 1, 1, halo_r, after=(snap,))
        edge = rows_of(state, q1, q2, after=back[-1:])
        halo = (state, q1, q2, *swap_y(*edge))
        snaps += [snap, q1, q2, snap_r, r1, r2]

    (receiver,) = back
    source, s1, s2 = run_block(BLOCKS - 1, 0, halo, (receiver,))
    final = [source, receiver, *swap_x(s1, s2)]

    noffsets = offsets.shape[0]
    wide = [TILE + 2 * HMAX, TILE, LANES]
    partial = call(
        functools.partial(image_kernel, BLOCKS - 1, True),
        "image",
        (struct(noffsets, TILE, TILE, LANES),),
        [SM, SM] + [VM] * (6 * (BLOCKS - 1)),
        scratch=[pltpu.VMEM((BLOCKS - 1, *wide), F32)] * 2,
    )(info, offsets, *snaps)
    outs = call(
        functools.partial(image_kernel, 1, False),
        "image_last",
        (struct(noffsets // groups, TILE, 8, LANES),) * groups,
        [SM, SM] + [VM] * 5,
        scratch=[pltpu.VMEM((1, *wide), F32)] * 2,
    )(info, offsets, partial[0], *final)
    parts = [outs[0]] + [
        lax.ppermute(outs[d], "grp", [(i, i ^ d) for i in range(groups)]) for d in range(1, groups)
    ]
    return call(
        gather_kernel,
        "gather",
        struct(noffsets // groups, TILE, TILE, 2 * LANES),
        [SM] + [VM] * 4,
        scratch=[pltpu.VMEM((groups, noffsets // groups, TILE, 8, LANES), F32)],
    )(info, *parts)


def solution(mesh):
    return jax.shard_map(
        shards,
        mesh=mesh,
        in_specs=(
            P(None, None, None, "gx", "gy", None),
            P("gx", "gy", None),
            P("gx", "gy", None),
            P("gx", "gy", None),
            P(),
            P(),
            P(),
        ),
        out_specs=P("grp", "gx", "gy", None),
        check_vma=False,
    )
```

```python
import functools

import jax
import jax.numpy as jnp
from jax import lax
from jax.experimental import pallas as pl
from jax.experimental.pallas import tpu as pltpu
from jax.sharding import PartitionSpec as P

NSTEPS = 16
SNAP = 4
MIRROR = True
HMAX = 8
BLOCKS = NSTEPS // SNAP
NW = 2
LANES = 128
TILE = 16
EXT = TILE + 2 * SNAP
YPAD = 8
YROWS = EXT + 2 * YPAD
FIELDS = ((0, 4, 0), (1, 3, 4), (2, 3, 7), (3, 2, 10))
ROWS = 12
FROWS = NW * ROWS
CROWS = 9
XROWS = 3 * FROWS // 4
GROUPED = 16
PARITY, LEFT, RIGHT, LOW, HIGH, START, FIRST, CHUNK, GROUP, BASE = range(10)
SENT = 3 * LANES // 4

VM = pl.BlockSpec(memory_space=pltpu.VMEM)
SM = pl.BlockSpec(memory_space=pltpu.SMEM)
F32 = jnp.float32


def struct(*shape, dtype=F32):
    return jax.ShapeDtypeStruct(shape, dtype)


def call(kernel, name, outs, in_specs, scratch=(), out_specs=None, cost=2_000_000, after=()):
    run = pl.pallas_call(
        lambda *refs: kernel(*refs[len(after) :]),
        out_shape=outs,
        in_specs=[pl.BlockSpec(memory_space=pl.ANY)] * len(after) + in_specs,
        out_specs=out_specs if out_specs is not None else jax.tree.map(lambda _: VM, outs),
        scratch_shapes=list(scratch),
        compiler_params=pltpu.CompilerParams(vmem_limit_bytes=16 << 20),
        cost_estimate=pl.CostEstimate(flops=cost, bytes_accessed=cost, transcendentals=0),
        name=name,
    )
    return functools.partial(run, *after)


def lane_iota(rows=8):
    return lax.broadcasted_iota(jnp.int32, (rows, LANES), 1)


def strips(info, state, width, rows, first, second):
    even = 1 - info[PARITY]
    far = TILE - width
    first[rows : rows + width] = state[pl.ds(even * far, width)]
    second[rows : rows + width] = state[pl.ds((1 - even) * far, width)]


def sides(info, first, second, row, whole=True):
    odd = info[PARITY] == 1
    if whole:
        a, b = first[row], second[row]
    else:
        a, b = unpacked(info, first, FROWS, row), unpacked(info, second, FROWS, row)
    left = jnp.where(odd, a, b)
    right = jnp.where(odd, b, a)
    zero = jnp.zeros_like(a)
    return jnp.where(info[LEFT] == 1, left, zero), jnp.where(info[RIGHT] == 1, right, zero)


def turned(info, block, by):
    return pltpu.roll(block, lax.rem(2 * LANES + by, LANES), block.ndim - 1)


def pack(info, source, out):
    n = source.shape[0] // 4
    wide = lax.broadcasted_iota(jnp.int32, (source.shape[1], LANES), 1) < SENT
    base = info[BASE]
    for i in range(n):
        for part in range(3):
            out[part * n + i] = jnp.where(
                wide,
                turned(info, source[part * n + i], -base),
                turned(info, source[3 * n + i], SENT - (LANES - SENT) * part - base),
            )


def unpacked(info, source, count, at):
    n = count // 4
    base = info[BASE]
    if at < 3 * n:
        return turned(info, source[at], base)
    rows = [source[part * n + at - 3 * n] for part in range(3)]
    lanes = lax.broadcasted_iota(jnp.int32, rows[0].shape, 1) - base
    step = LANES - SENT
    a, b, c = (turned(info, row, base - SENT + step * part) for part, row in enumerate(rows))
    return jnp.where(lanes < step, a, jnp.where(lanes < 2 * step, b, c))


def window(info, block):
    start = info[START]
    shift = lax.rem(LANES - start, LANES)
    return jnp.where(
        lane_iota(TILE) < LANES - start,
        pltpu.roll(block[:, :LANES], shift, 1),
        pltpu.roll(block[:, LANES:], shift, 1),
    )


def prepare_coef(info, model, coef, c1, c2):
    for x in range(TILE):
        c, e, d = (window(info, model[k, x]) for k in range(3))
        coef[0, x] = c + 2.0 * c * e
        coef[1, x] = c * jnp.sqrt(2.0 * d + 1.0)
        coef[2, x] = c
    for k in range(3):
        strips(info, coef.at[k], 3, 3 * k, c1, c2)


def prepare_state(info, check, state, s1, s2, lay1, lay2):
    for w in range(NW):
        for f, width, row in FIELDS:
            for x in range(TILE):
                state[w, f, x] = window(info, check[w, f // 2, f % 2, x])
            strips(info, state.at[w, f], width, w * ROWS + row, lay1, lay2)
    pack(info, lay1, s1)
    pack(info, lay2, s2)


def listing(most, code, cells, count):
    for row in range(code.shape[0]):

        def some(group, n):
            def each(n):
                for i in range(GROUPED):
                    value = code[row, group * GROUPED + i]
                    cells[row, n] = value
                    n = n + jnp.where(value >= 0, 1, 0)
                return n

            return lax.cond(most[row, group] >= 0, each, lambda n: n, n)

        count[row] = lax.fori_loop(0, code.shape[1] // GROUPED, some, jnp.int32(0))


def coef_whole(info, coef, r1, r2, below, above, out):
    out[...] = jnp.zeros_like(out)
    for k in range(3):
        out[k, SNAP : SNAP + TILE, SNAP : SNAP + TILE] = coef[k]
        for row in range(3):
            left, right = sides(info, r1, r2, 3 * k + row)
            out[k, 1 + row, SNAP : SNAP + TILE] = left
            out[k, SNAP + TILE + row, SNAP : SNAP + TILE] = right
        for x in range(1, EXT - 1):
            at = x * CROWS + 3 * k
            lo = below[at : at + 3]
            hi = above[at : at + 3]
            out[k, x, 1:4] = jnp.where(info[LOW] == 1, lo, jnp.zeros_like(lo))
            out[k, x, SNAP + TILE : SNAP + TILE + 3] = jnp.where(info[HIGH] == 1, hi, jnp.zeros_like(hi))


def field_rows(info, state, r1, r2, low, high, low_rows, high_rows):
    own = [(state.at[w, f], width, w * ROWS + row) for w in range(NW) for f, width, row in FIELDS]
    edge_rows(info, own, FROWS, False, r1, r2, low_rows, high_rows)
    for rows, out in ((low_rows, low), (high_rows, high)):
        pack(info, rows.reshape(EXT * FROWS // 8, 8, LANES), out)


def coef_rows(info, coef, r1, r2, low, high):
    edge_rows(info, [(coef.at[k], 3, 3 * k) for k in range(3)], CROWS, True, r1, r2, low, high)


def edge_rows(info, arrays, stride, whole, r1, r2, low, high):
    for own, width, row in arrays:
        for n in range(width):
            left, right = sides(info, r1, r2, row + n, whole)
            for x, layer in ((SNAP - width + n, left), (SNAP + TILE + n, right)):
                at = x * stride + row
                low[at : at + width] = layer[:width]
                high[at : at + width] = layer[TILE - width :]
        for x in range(TILE):
            at = (x + SNAP) * stride + row
            low[at : at + width] = own[x, :width]
            high[at : at + width] = own[x, TILE - width :]
        for x in [*range(SNAP - width), *range(EXT - SNAP + width, EXT)]:
            at = x * stride + row
            low[at : at + width] = jnp.zeros((width, LANES), F32)
            high[at : at + width] = jnp.zeros((width, LANES), F32)


def block_kernel(chain, has_state, last, *refs):
    refs = list(refs)
    info, cells, count, amps, coef = refs[:5]
    refs = refs[5:]
    if has_state:
        state, r1, r2, below, above = refs[:5]
        refs = refs[5:]
    if not last:
        out_state, refs = refs[0], refs[1:]
    snap, s1, s2 = refs[:3]
    refs = refs[3:]
    bufs = refs[:4]
    lay1, lay2, below_rows, above_rows = refs[4:]
    own = slice(YPAD + SNAP, YPAD + SNAP + TILE)
    if has_state:
        for rows_in, rows_out in ((below, below_rows), (above, above_rows)):
            for i in range(EXT * FROWS // 8):
                rows_out[8 * i : 8 * i + 8] = unpacked(info, rows_in, EXT * FROWS // 8, i)
        for w in range(NW):
            for f, width, row in FIELDS:
                at = w * ROWS + row
                bufs[f][w, SNAP : SNAP + TILE, own] = state[w, f]
                for n in range(width):
                    left, right = sides(info, r1, r2, at + n, False)
                    bufs[f][w, SNAP - width + n, own] = left
                    bufs[f][w, SNAP + TILE + n, own] = right
                for x in range(SNAP - width, SNAP + TILE + width):
                    lo = below_rows[x * FROWS + at : x * FROWS + at + width]
                    hi = above_rows[x * FROWS + at : x * FROWS + at + width]
                    bufs[f][w, x, YPAD + SNAP - width : YPAD + SNAP] = jnp.where(
                        info[LOW] == 1, lo, jnp.zeros_like(lo)
                    )
                    bufs[f][w, x, YPAD + SNAP + TILE : YPAD + SNAP + TILE + width] = jnp.where(
                        info[HIGH] == 1, hi, jnp.zeros_like(hi)
                    )
    else:
        for buf in bufs:
            buf[...] = jnp.zeros_like(buf)

    lanes = lane_iota()
    bottom, top = lanes == 0, lanes == LANES - 1
    one_row = lane_iota(1)
    for step in range(SNAP):
        extent = SNAP - 1 - step
        now, then = (bufs[:2], bufs[2:]) if step % 2 == 0 else (bufs[2:], bufs[:2])
        main, aux = now
        main_next, aux_next = then

        def layer(x):
            for chunk in range(EXT // 8):
                at = YPAD + 8 * chunk
                mid = pl.ds(at, 8)
                horizontal = coef[0, x, 8 * chunk : 8 * chunk + 8]
                coupling = coef[1, x, 8 * chunk : 8 * chunk + 8]
                vertical = coef[2, x, 8 * chunk : 8 * chunk + 8]
                for w in range(NW):
                    m = main[w, x, mid]
                    across = (
                        (main[w, x + 1, mid] + main[w, x - 1, mid])
                        + (main[w, x, pl.ds(at + 1, 8)] + main[w, x, pl.ds(at - 1, 8)])
                        - 4.0 * m
                    )
                    a = aux[w, x, mid]
                    deeper = jnp.where(top, 0.0, pltpu.roll(a, LANES - 1, 1))
                    upper = jnp.where(bottom, 0.0, pltpu.roll(a, 1, 1))
                    down = deeper + upper - 2.0 * a
                    main_next[w, x, mid] = (
                        2.0 * m - main_next[w, x, mid] + (horizontal * across + coupling * down)
                    )
                    aux_next[w, x, mid] = (
                        2.0 * a - aux_next[w, x, mid] + (coupling * across + vertical * down)
                    )

        for x in range(SNAP - extent, SNAP + TILE + extent):
            layer(x)
        for w in range(NW):

            def inject(i, carry):
                cell = cells[chain + 2 * w, i]
                amount = amps[w, step, lax.shift_right_logical(cell, 18)]
                x = lax.bitwise_and(lax.shift_right_logical(cell, 13), 31)
                y = lax.bitwise_and(lax.shift_right_logical(cell, 7), 63)
                z = lax.bitwise_and(cell, LANES - 1)
                add = jnp.where(one_row == z, amount, 0.0)
                main_next[w, x, pl.ds(y, 1)] += add
                aux_next[w, x, pl.ds(y, 1)] += add
                return carry

            lax.fori_loop(0, count[chain + 2 * w], inject, 0)

    for x in range(TILE):
        snap[x] = packed(info, bufs[0][0, x + SNAP, own], bufs[0][1, x + SNAP, own])
    if not last:
        for w in range(NW):
            for f, width, row in FIELDS:
                out_state[w, f] = bufs[f][w, SNAP : SNAP + TILE, own]
                strips(info, out_state.at[w, f], width, w * ROWS + row, lay1, lay2)
        pack(info, lay1, s1)
        pack(info, lay2, s2)
        even = 1 - info[PARITY]
        s1[XROWS:] = snap[pl.ds(SNAP + SNAP * even, HMAX - SNAP)]
        s2[XROWS:] = snap[pl.ds(SNAP + SNAP * (1 - even), HMAX - SNAP)]
    else:
        strips(info, snap, HMAX, 0, s1, s2)


def packed(info, first, second):
    to_left = lax.rem(LANES - info[FIRST], LANES)
    to_right = lax.rem(LANES + LANES // 2 - info[FIRST], LANES)
    return jnp.where(
        lane_iota(TILE) < LANES // 2, pltpu.roll(first, to_left, 1), pltpu.roll(second, to_right, 1)
    )


def widen_far(info, own, r1, r2, out):
    out[HMAX : HMAX + TILE] = own[...]
    for row in range(HMAX):
        left, right = sides(info, r1, r2, row)
        out[row] = left
        out[HMAX + TILE + row] = right


def widen(info, own, r1, r2, out):
    out[HMAX : HMAX + TILE] = own[...]
    for row in range(SNAP):
        left, right = sides(info, r1, r2, XROWS + row)
        out[row] = left
        out[HMAX + TILE + SNAP + row] = right
        ends = [sides(info, r1, r2, w * ROWS + row, False) for w in range(NW)]
        out[SNAP + row] = packed(info, ends[0][0], ends[1][0])
        out[HMAX + TILE + row] = packed(info, ends[0][1], ends[1][1])


def image_kernel(count, first, *refs):
    refs = list(refs)
    info, offsets = refs[:2]
    refs = refs[2:]
    if not first:
        before, refs = refs[0], refs[1:]
    snaps, refs = refs[: 6 * count], refs[6 * count :]
    outs, (source, receiver) = refs[:-2], refs[-2:]
    if first:
        for j in range(count):
            widen(info, *snaps[6 * j : 6 * j + 3], source.at[j])
            widen(info, *snaps[6 * j + 3 : 6 * j + 6], receiver.at[j])
    else:
        widen_far(info, *snaps[:3], source.at[0])
        widen_far(info, *snaps[3:], receiver.at[0])
    half = lax.broadcasted_iota(jnp.int32, (TILE, 8, LANES), 2) < LANES // 2
    group = info[GROUP]
    for d in range(4):
        for i in range(4):
            shift = offsets[4 * lax.bitwise_xor(group, d) + i]

            at_source = pl.ds(HMAX - shift, TILE)
            at_receiver = pl.ds(HMAX + shift, TILE)
            sums = []
            for y in range(2):
                rows = slice(8 * y, 8 * y + 8)
                total = source[0, at_source, rows] * receiver[0, at_receiver, rows]
                for j in range(1, count):
                    total += source[j, at_source, rows] * receiver[j, at_receiver, rows]
                if not first:
                    total += before[4 * d + i, :, rows]
                sums.append(total)
            if first:
                for y in range(2):
                    outs[0][4 * d + i, :, 8 * y : 8 * y + 8] = sums[y]
            else:
                a, b = (t + pltpu.roll(t, LANES // 2, 2) for t in sums)
                outs[d][i] = jnp.where(half, a, b)


def gather_kernel(info, *refs):
    parts, out, held = refs[:4], refs[4], refs[5]
    for d in range(4):
        held[d] = parts[d][...]
    half = lax.broadcasted_iota(jnp.int32, (TILE, 8, LANES), 2) < LANES // 2
    mine = info[CHUNK]
    for tile in range(2):
        low = lax.bitwise_xor(mine, 2 * tile)
        high = lax.bitwise_xor(mine, 2 * tile + 1)
        at = slice(tile * LANES, (tile + 1) * LANES)
        for i in range(4):
            a = held[low, i]
            b = held[high, i]
            out[i, :, 0:8, at] = jnp.where(half, a, pltpu.roll(b, LANES // 2, 2))
            out[i, :, 8:16, at] = jnp.where(half, pltpu.roll(a, LANES // 2, 2), b)


def shards(checkpoint, courant, epsilon, delta, positions, amplitudes, offsets):
    group, gx, gy = (lax.axis_index(axis) for axis in ("grp", "gx", "gy"))
    groups, nx, ny = (lax.axis_size(axis) for axis in ("grp", "gx", "gy"))
    quarter = courant.shape[2] // groups
    far = (gx // 2) % 2
    chunk = jnp.where(far == 1, groups - 1 - group, group) if MIRROR else group
    start = jnp.clip(quarter * chunk - quarter // 2, 0, courant.shape[2] - LANES)
    info = jnp.stack(
        [
            gx % 2,
            (gx > 0).astype(jnp.int32),
            (gx < nx - 1).astype(jnp.int32),
            (gy > 0).astype(jnp.int32),
            (gy < ny - 1).astype(jnp.int32),
            start,
            quarter * chunk - start,
            chunk,
            group,
            (quarter * chunk - start) // 2,
        ]
    ).astype(jnp.int32)

    pair = [(i, i ^ 1) for i in range(nx)]
    other = [(i, ((i - 1) % nx ^ 1) + 1) for i in range(nx)]
    other = [(i, j % nx) for i, j in other]

    mirrored = [
        (g * nx + i, (groups - 1 - g) * nx + j) for g in range(groups) for i, j in other
    ]

    def swap_x(first, second):
        back = lax.ppermute(first, "gx", pair)
        if MIRROR:
            return back, lax.ppermute(second, ("grp", "gx"), mirrored)
        return back, lax.ppermute(second, "gx", other)

    def swap_y(low, high):
        below = lax.ppermute(high, "gy", [(i, (i + 1) % ny) for i in range(ny)])
        above = lax.ppermute(low, "gy", [(i, (i - 1) % ny) for i in range(ny)])
        return below, above

    local_x = positions[:, 0] - gx * TILE + SNAP
    local_y = positions[:, 1] - gy * TILE + SNAP
    local_z = positions[:, 2] - start
    inside = (local_x >= 1) & (local_x < EXT - 1) & (local_y >= 1) & (local_y < EXT - 1)
    inside &= (local_z >= 0) & (local_z < LANES)
    cell = (local_x << 13) | ((local_y + YPAD) << 7) | local_z
    point = jnp.arange(positions.shape[2], dtype=jnp.int32) << 18
    code = jnp.where(inside, point | cell, -1)
    npoints = code.shape[1]

    rows = code.shape[0]
    lists = call(
        listing,
        "listing",
        (
            struct(rows, npoints, dtype=jnp.int32),
            struct(rows, dtype=jnp.int32),
        ),
        [SM, SM],
        out_specs=(SM, SM),
    )(code.reshape(rows, npoints // GROUPED, GROUPED).max(axis=2), code)
    layers = [pltpu.VMEM((FROWS, TILE, LANES), F32)] * 2
    rows_whole = [pltpu.VMEM((EXT * FROWS, LANES), F32)] * 2
    rows_sent = struct(3 * EXT * FROWS // 32, 8, LANES)
    coef, c1, c2 = call(
        prepare_coef,
        "prepare_coef",
        (struct(3, TILE, TILE, LANES), struct(CROWS, TILE, LANES), struct(CROWS, TILE, LANES)),
        [SM, VM],
    )(info, jnp.stack([courant, epsilon, delta]))
    c1, c2 = swap_x(c1, c2)
    coef_edge = call(
        coef_rows,
        "coef_rows",
        (struct(CROWS * EXT, LANES),) * 2,
        [SM] + [VM] * 3,
        after=lists[1:],
    )(info, coef, c1, c2)
    state, s1, s2 = call(
        prepare_state,
        "prepare_state",
        (
            struct(NW, 4, TILE, TILE, LANES),
            struct(XROWS, TILE, LANES),
            struct(XROWS, TILE, LANES),
        ),
        [SM, VM],
        scratch=layers,
        after=coef_edge[:1],
    )(info, checkpoint)

    def rows_of(own, r1, r2, after=()):
        return call(
            field_rows,
            "field_rows",
            (rows_sent, rows_sent),
            [SM] + [VM] * 3,
            scratch=rows_whole,
            after=after,
        )(info, own, r1, r2)

    below, above = swap_y(*coef_edge)
    r1, r2 = swap_x(s1, s2)
    edge = rows_of(state, r1, r2, after=coef_edge[:1])
    halo = (state, r1, r2, *swap_y(*edge))
    coef = call(coef_whole, "coef_whole", struct(3, EXT, EXT, LANES), [SM] + [VM] * 5)(
        info, coef, c1, c2, below, above
    )

    def run_block(number, chain, halo, after=()):
        last = number == BLOCKS - 1
        amps = amplitudes[chain::2, number * SNAP : (number + 1) * SNAP]
        strip = struct(HMAX if last else XROWS + HMAX - SNAP, TILE, LANES)
        outs = [struct(TILE, TILE, LANES), strip, strip]
        if not last:
            outs = [struct(NW, 4, TILE, TILE, LANES), *outs]
        return call(
            functools.partial(block_kernel, chain, bool(halo), last),
            "block",
            tuple(outs),
            [SM] * 4 + [VM] * (1 + len(halo)),
            scratch=[pltpu.VMEM((NW, EXT, YROWS, LANES), F32)] * 4 + layers + rows_whole,
            cost=8_000_000,
            after=after,
        )(info, *lists, amps, coef, *halo)

    snaps = []
    back = run_block(0, 1, ())
    for number in range(BLOCKS - 1):
        state_r, snap_r, *strips_r = back
        r1, r2 = swap_x(*strips_r)
        edge_r = rows_of(state_r, r1, r2, after=edge[:1])
        halo_r = (state_r, r1, r2, *swap_y(*edge_r))
        gate = edge_r[:1] if number else ()
        state, snap, *strips_s = run_block(number, 0, halo, after=gate)
        q1, q2 = swap_x(*strips_s)
        back = run_block(number + 1, 1, halo_r, after=(snap,))
        edge = rows_of(state, q1, q2, after=back[-1:])
        halo = (state, q1, q2, *swap_y(*edge))
        snaps += [snap, q1, q2, snap_r, r1, r2]

    receiver, s1, s2 = back
    final = [receiver, *swap_x(s1, s2)]
    source, s1, s2 = run_block(BLOCKS - 1, 0, halo)
    final = [source, *swap_x(s1, s2), *final]

    noffsets = offsets.shape[0]
    wide = [TILE + 2 * HMAX, TILE, LANES]
    partial = call(
        functools.partial(image_kernel, BLOCKS - 1, True),
        "image",
        (struct(noffsets, TILE, TILE, LANES),),
        [SM, SM] + [VM] * (6 * (BLOCKS - 1)),
        scratch=[pltpu.VMEM((BLOCKS - 1, *wide), F32)] * 2,
    )(info, offsets, *snaps)
    outs = call(
        functools.partial(image_kernel, 1, False),
        "image_last",
        (struct(noffsets // groups, TILE, 8, LANES),) * groups,
        [SM, SM] + [VM] * 7,
        scratch=[pltpu.VMEM((1, *wide), F32)] * 2,
    )(info, offsets, partial[0], *final)
    parts = [outs[0]] + [
        lax.ppermute(outs[d], "grp", [(i, i ^ d) for i in range(groups)]) for d in range(1, groups)
    ]
    return call(
        gather_kernel,
        "gather",
        struct(noffsets // groups, TILE, TILE, 2 * LANES),
        [SM] + [VM] * 4,
        scratch=[pltpu.VMEM((groups, noffsets // groups, TILE, 8, LANES), F32)],
    )(info, *parts)


def solution(mesh):
    return jax.shard_map(
        shards,
        mesh=mesh,
        in_specs=(
            P(None, None, None, "gx", "gy", None),
            P("gx", "gy", None),
            P("gx", "gy", None),
            P("gx", "gy", None),
            P(),
            P(),
            P(),
        ),
        out_specs=P("grp", "gx", "gy", None),
        check_vma=False,
    )
```
